32 devices in a mesh: pulse: 4 (over z), tile: 8 (over y, x, core).
Axes of the slice: x: 2, y: 2, z: 4, core: 2. Of those that a mesh axis runs over, the one named last changes fastest.
Arguments:
- raw: bfloat16 [2, 128, 2048], P(None, ('pulse', 'tile')), may hold values from -6 to 6
- filt: bfloat16 [2, 1024, 2048], replicated, may hold values from -0.125 to 0.125
- range_off: int32 [128], P(('pulse', 'tile')), may hold values from 0 to 1024
- fine: int32 [128], P(('pulse', 'tile')), may hold values from 0 to 3
- dop: int32 [128], P(('pulse', 'tile')), may hold values from 0 to 511
- pulse_order: int32 [32, 4], P(('pulse', 'tile')), may hold values from 0 to 3, each once within a row
- band_idx: int32 [8, 128], P(None, ('pulse', 'tile')), may hold values from 0 to 1023
Outputs:
- image: bfloat16 [2, 512, 32768], P(None, 'pulse', 'tile')
The draws below stay inside these ranges and needn't reach their ends.
Inputs may be any that keep to these rules, and one draw needn't show every extreme that they name: `pulse_order`: each row is a permutation of 0 .. 3.
All inputs are finite; a program needn't handle non-finite values.
Results may differ from the reference program's by a relative error of at most 0.0065.
Values may be sent and summed in bfloat16 or wider, within the bound.
A program may use at most 192 MiB of HBM per device.

```python
import jax
import jax.numpy as jnp
from jax import lax

RAW = 2048
WIN = 1024
UPS = 2048
BAND = 1024
STEPS = 4
PS = 1
C_T = 4096
P_DEV = 4
PULSES = 128
ROWS = 512
N_TILE = 8
DEVICES = 32


def place_ends(result, rng, low, top_value):
    dims = result.shape
    spot = [jax.random.randint(jax.random.fold_in(rng, axis), (), 0, dims[axis]) for axis in range(len(dims))]
    result = result.at[tuple(spot)].set(low)
    longest = dims.index(max(dims))
    spot[longest] = (spot[longest] + 1) % dims[longest]
    return result.at[tuple(spot)].set(top_value)


def block_scale(key, extent, shards, smallest, top_value):
    gain, own = 1.0, jax.random.fold_in(key, 6)
    for dim, parts in shards:
        draws = jnp.exp(jax.random.uniform(jax.random.fold_in(own, dim), (parts,), jnp.float32, smallest / len(shards), top_value / len(shards)))
        gain = gain * jnp.repeat(draws, extent[dim] // parts).reshape([-1 if axis == dim else 1 for axis in range(len(extent))])
    return gain


def gaussian(stream_key, extent, deviation, most, split=(), held_as=jnp.bfloat16):
    result = deviation * jax.random.normal(stream_key, extent, jnp.float32)
    if split:
        result = result * block_scale(stream_key, extent, split, -0.22, 0.18)
    return jnp.clip(result, -most, most).astype(held_as)


def setup_inputs(seed: int = 0) -> dict:
    seeds = jax.random.split(jax.random.key(seed), 8)
    return {
        "raw": gaussian(seeds[0], (2, PULSES, RAW), 1.0, 6.0, ((1, 32),)),
        "filt": gaussian(seeds[1], (2, WIN, UPS), (2 * WIN) ** -0.5, 0.125),
        "range_off": place_ends(jax.random.randint(seeds[2], (PULSES,), 0, RAW - WIN + 1), jax.random.fold_in(seeds[2], 1), 0, RAW - WIN).astype(jnp.int32),
        "fine": place_ends(jax.random.randint(seeds[3], (PULSES,), 0, 4), jax.random.fold_in(seeds[3], 1), 0, 3).astype(jnp.int32),
        "dop": place_ends(jax.random.randint(seeds[4], (PULSES,), 0, ROWS), jax.random.fold_in(seeds[4], 1), 0, ROWS - 1).astype(jnp.int32),
        "pulse_order": jax.vmap(lambda own: jax.random.permutation(own, P_DEV))(jax.random.split(seeds[5], DEVICES)).reshape((DEVICES, P_DEV)).astype(jnp.int32),
        "band_idx": place_ends(jax.random.randint(seeds[6], (N_TILE, PULSES), 0, UPS - BAND), jax.random.fold_in(seeds[6], 1), 0, (UPS - BAND) - 1).astype(jnp.int32),
    }


def compress(windows, filt):
    wr = windows[:, 0]
    wi = windows[:, 1]
    prof_re = jnp.dot(wr, filt[0], preferred_element_type=jnp.float32) - jnp.dot(wi, filt[1], preferred_element_type=jnp.float32)
    prof_im = jnp.dot(wr, filt[1], preferred_element_type=jnp.float32) + jnp.dot(wi, filt[0], preferred_element_type=jnp.float32)
    return jnp.stack([prof_re, prof_im], 1).astype(jnp.bfloat16)

def cut_band(profile, start):
    segment = lax.dynamic_slice_in_dim(profile, start, BAND + 1, 1)
    return (segment[:, :BAND], segment[:, BAND])

def interpolate(pieces, edges, shifts):
    first = pieces.astype(jnp.float32)
    second = jnp.concatenate([first[..., 1:], edges.astype(jnp.float32)[..., None]], -1)
    first = jnp.repeat(first, 4, axis=-1)
    second = jnp.repeat(second, 4, axis=-1)
    phase_q = (jnp.arange(4 * BAND, dtype=jnp.int32) % 4).astype(jnp.float32)
    weight = (4.0 * phase_q[None, :] + shifts.astype(jnp.float32)[:, None]) / 16.0
    weight = weight[:, None, :]
    return first * (1.0 - weight) + second * weight

def reference(raw, filt, range_off, fine, dop, pulse_order, band_idx):
    devices = pulse_order.shape[0]
    p_dev = pulse_order.shape[1]
    pulses = p_dev * devices
    owners = jnp.arange(devices, dtype=jnp.int32)[:, None] * p_dev
    rows = jnp.arange(ROWS, dtype=jnp.int32)
    lefts = []
    rights = []
    for step in range(STEPS):
        chosen = (owners + pulse_order[:, step * PS:(step + 1) * PS]).reshape(-1).astype(jnp.int32)
        picked = jnp.take(raw, chosen, axis=1)
        offsets = jnp.take(range_off, chosen)
        windows = jax.vmap(lambda row, off: lax.dynamic_slice_in_dim(row, off, WIN, 1), in_axes=(1, 0))(picked, offsets)
        profile = compress(windows, filt)
        starts = jnp.take(band_idx, chosen, axis=1)
        shifts = jnp.take(fine, chosen)
        pieces, edges = jax.vmap(jax.vmap(cut_band, in_axes=(0, 0)), in_axes=(None, 0))(profile, starts)
        samples = jax.vmap(interpolate, in_axes=(0, 0, None))(pieces, edges, shifts)
        summed = lax.optimization_barrier(jnp.sum(samples, axis=1))
        sr = samples[:, :, 0]
        si = samples[:, :, 1]
        rr = summed[:, None, 0]
        ri = summed[:, None, 1]
        g_re = lax.optimization_barrier(jnp.sum(sr * rr + si * ri, axis=(0, 2)))
        g_im = lax.optimization_barrier(jnp.sum(si * rr - sr * ri, axis=(0, 2)))
        scale = jnp.sqrt(g_re * g_re + g_im * g_im + 1.0)
        c_re = (g_re / scale)[None, :, None]
        c_im = (-g_im / scale)[None, :, None]
        new_re = c_re * sr - c_im * si
        new_im = c_re * si + c_im * sr
        rights.append(jnp.concatenate([new_re, new_im], 1).astype(jnp.bfloat16))
        dops = jnp.take(dop, chosen)
        angle = 2.0 * jnp.pi * (dops[:, None] * rows[None, :] % ROWS).astype(jnp.float32) / ROWS
        e_re = (jnp.cos(angle) / jnp.sqrt(jnp.float32(pulses))).astype(jnp.bfloat16)
        e_im = (jnp.sin(angle) / jnp.sqrt(jnp.float32(pulses))).astype(jnp.bfloat16)
        lefts.append(jnp.stack([jnp.concatenate([e_re, -e_im], 0), jnp.concatenate([e_im, e_re], 0)], 0))
    left_all = jnp.concatenate(lefts, 1).astype(jnp.float32)
    right_all = jnp.concatenate(rights, 1)

    def one_tile(right):
        return jnp.einsum('zkr,kc->zrc', left_all, right.astype(jnp.float32)).astype(jnp.bfloat16)
    tiles = lax.map(one_tile, right_all)
    n_tile = tiles.shape[0]
    return jnp.transpose(tiles, (1, 2, 0, 3)).reshape(2, ROWS, n_tile * C_T)
```

```python
import functools

import jax
import jax.numpy as jnp
from jax import lax
from jax.experimental import pallas as pl
from jax.experimental.pallas import tpu as pltpu
from jax.sharding import PartitionSpec as P

F32 = jnp.float32
BF16 = jnp.bfloat16
MESH = pl.DeviceIdType.MESH
LANES = 128
DOP_SPLIT = 32
VMEM_LIMIT = 44 * 1024 * 1024
IMAGE_VMEM = 16 * 1024 * 1024


def spread(meta, field, rows8, n_rows):
    lane = lax.broadcasted_iota(jnp.int32, (meta.shape[1], n_rows), 0)
    col = lax.broadcasted_iota(jnp.int32, (meta.shape[1], n_rows), 1)
    pick = (lane == field * rows8 + col % rows8).astype(F32).astype(BF16)
    wide = jnp.dot(meta, pick, preferred_element_type=F32)
    owner = lax.broadcasted_iota(jnp.int32, wide.shape, 0)
    column = lax.broadcasted_iota(jnp.int32, wide.shape, 1)
    return jnp.sum(jnp.where(owner == column // rows8, wide, 0.0), axis=0, keepdims=True)


def thirds(x):
    a = x.astype(BF16)
    rest = x - a.astype(F32)
    b = rest.astype(BF16)
    return [a, b, (rest - b.astype(F32)).astype(BF16)]


def swap_parts(v, part1, p_dev):
    n = v.shape[-1]
    return jnp.where(part1, pltpu.roll(v, p_dev, 1), pltpu.roll(v, n - p_dev, 1))


def focus_kernel(
    n_pulse, n_tile, r_dev,
    off_in, fine_in, dop_in, order_in, idx_in, raw_in, filt_ref,
    left_ref, samp_ref,
    off_ref, fine_ref, dop_ref, order_ref, idx_ref, raw_ref,
    bands_ref, up_ref, win_ref, meta_ref, scal_ref, filt_buf, x_ref, prof_ref, cut_ref, out_buf, g_ref, got_ref,
    i_sem, f_sem, s_sem, z_send, z_recv, t_send, t_recv, p_send, p_recv, g_send, g_recv,
):
    me_p = lax.axis_index("pulse")
    me_t = lax.axis_index("tile")
    half = n_tile // 2
    core = me_t % 2
    chip = me_t // 2
    partner = chip * 2 + (1 - core)
    p_dev = raw_ref.shape[1]
    steps = order_ref.shape[1]
    raw_len = raw_ref.shape[2]
    win = x_ref.shape[2]
    rows = x_ref.shape[1]
    rows8 = 2 * p_dev
    n_dev = n_pulse * half
    n_rows = 2 * rows
    chunks, chunk = filt_buf.shape[0], filt_buf.shape[3]
    stride = prof_ref.shape[0] // rows
    ext = bands_ref.shape[2]
    band = ext - LANES
    pieces = band // LANES

    def pulse_at(i):
        low, high = me_p, n_pulse - 1 - me_p
        both = jnp.minimum(low, high)
        two_sided = i <= 2 * both
        dist = jnp.where(two_sided, (i + 1) // 2, i - both)
        up = jnp.where(two_sided, i % 2, jnp.where(high > low, 1, 0))
        return me_p + (2 * up - 1) * dist

    def pulse_peer(d):
        return (lax.rem(me_p + d, n_pulse), me_t)

    def flip(k):
        bits = [1 << n for n in range(half.bit_length() - 1)]
        return sum(((chip // b + k // b) % 2) * b for b in bits)

    def tile_peer(k):
        return (me_p, flip(k) * 2 + core)

    def any_tile(d):
        return (me_p, lax.rem(me_t + d, n_tile))

    barrier = pltpu.get_barrier_semaphore()
    for d in range(1, n_pulse):
        pl.semaphore_signal(barrier, 1, device_id=pulse_peer(d), device_id_type=MESH)
    for d in range(1, n_tile):
        pl.semaphore_signal(barrier, 1, device_id=any_tile(d), device_id_type=MESH)

    def load_filter(n):
        return pltpu.make_async_copy(
            filt_ref.at[:, :, pl.ds(n * chunk, chunk)], filt_buf.at[n], f_sem.at[n]
        )

    inputs = [
        pltpu.make_async_copy(src, dst, i_sem.at[n])
        for n, (src, dst) in enumerate(
            [(raw_in, raw_ref), (off_in, off_ref), (order_in, order_ref)]
            + [(fine_in, fine_ref), (dop_in, dop_ref), (idx_in, idx_ref)]
        )
    ]
    for copy in inputs:
        copy.start()
    for n in range(chunks):
        load_filter(n).start()
    for copy in inputs:
        copy.wait()

    raw = jnp.concatenate([raw_ref[0].astype(F32), raw_ref[1].astype(F32)], 0)
    row = lax.broadcasted_iota(jnp.int32, (rows8, win), 0)
    cut = jnp.zeros((rows8, win), F32)
    for p in range(p_dev):
        off = off_ref[p]
        shift = jnp.where(off == 0, 0, raw_len - off)
        turned = pltpu.roll(raw, shift, 1)[:, :win]
        cut = jnp.where(row % p_dev == p, turned, cut)
    mine = me_p * half + chip
    win_ref[mine] = cut.astype(BF16)
    lane = lax.broadcasted_iota(jnp.int32, meta_ref.shape[2:], 1)
    line = jnp.zeros(meta_ref.shape[2:], jnp.int32)
    for p in range(p_dev):
        pulse_lane = (lane < 4 * rows8) & (lane % p_dev == p)
        line = jnp.where(pulse_lane & (lane // rows8 == 1), fine_ref[p], line)
        line = jnp.where(pulse_lane & (lane // rows8 == 2), dop_ref[p] % DOP_SPLIT, line)
        line = jnp.where(pulse_lane & (lane // rows8 == 3), dop_ref[p] // DOP_SPLIT, line)
        line = jnp.where((lane < rows8) & (lane % p_dev == order_ref[0, p]), p, line)
        for t in range(n_tile):
            line = jnp.where(lane == 4 * rows8 + t * p_dev + p, idx_ref[p, t], line)
    meta_ref[core, mine] = line
    j = lax.broadcasted_iota(jnp.int32, up_ref.shape, 0)
    c = lax.broadcasted_iota(jnp.int32, up_ref.shape, 1)
    w = (c % 4).astype(F32) * 0.25
    up = jnp.where(j < LANES, 1.0 - w, w)
    up_ref[...] = jnp.where(j % LANES == c // 4, up, 0.0).astype(BF16)
    pl.semaphore_wait(barrier, n_pulse - 1 + n_tile - 1)

    def copies(slot, send, recv, at, target):
        return [
            pltpu.make_async_remote_copy(
                src_ref=ref, dst_ref=ref, send_sem=send.at[(a,) + at], recv_sem=recv.at[(a,) + at],
                device_id=target, device_id_type=MESH,
            )
            for a, ref in enumerate((win_ref.at[slot], meta_ref.at[core, slot]))
        ]

    started = []

    def send(*args):
        for c in copies(*args):
            c.start()
            started.append(c)

    def arrive(*args):
        for c in copies(*args):
            c.wait_recv()

    nearest = [pulse_at(i) for i in range(1, n_pulse)]
    for q in reversed(nearest):
        d = lax.rem(q - me_p + n_pulse, n_pulse)
        send(mine, z_send, z_recv, (d,), (q, me_t))
    for q in [me_p] + nearest:
        dp = lax.rem(me_p - q + n_pulse, n_pulse)
        slot = q * half + chip
        if q is not me_p:
            arrive(slot, z_send, z_recv, (dp,), (q, me_t))
        for k in reversed(range(1, half)):
            send(slot, t_send, t_recv, (dp, k), tile_peer(k))
    for q in [me_p] + nearest:
        dp = lax.rem(me_p - q + n_pulse, n_pulse)
        for k in range(1, half):
            arrive(q * half + flip(k), t_send, t_recv, (dp, k), tile_peer(k))

    to_scalar = pltpu.make_async_copy(meta_ref.at[core], scal_ref, s_sem)
    to_scalar.start()
    meta_move = pltpu.make_async_remote_copy(
        src_ref=meta_ref.at[core], dst_ref=meta_ref.at[core],
        send_sem=p_send.at[2], recv_sem=p_recv.at[2],
        device_id=(me_p, partner), device_id_type=MESH,
    )
    meta_move.start()
    for n in range(chunks):
        load_filter(n).wait()
    x = win_ref[...].astype(F32)
    r = lax.broadcasted_iota(jnp.int32, x.shape, 1)
    y = jnp.where(r < p_dev, -1.0, 1.0) * pltpu.roll(x, p_dev, 1)
    x_ref[0] = x.reshape(rows, win).astype(BF16)
    x_ref[1] = y.reshape(rows, win).astype(BF16)

    for n in range(chunks):
        acc = jnp.dot(x_ref[0], filt_buf[n, 0], preferred_element_type=F32) + jnp.dot(
            x_ref[1], filt_buf[n, 1], preferred_element_type=F32
        )
        for c in range(chunk // LANES):
            prof_ref[pl.ds(n * (chunk // LANES) + c, rows, stride=stride), :] = acc[
                :, c * LANES : (c + 1) * LANES
            ]
    to_scalar.wait()
    lane8 = lax.broadcasted_iota(jnp.int32, (pieces, LANES), 1)

    def cut_bands(tile, part_of):
        def owner(d, carry):
            for p in range(p_dev):
                start = scal_ref[d, 0, 4 * rows8 + tile * p_dev + p]
                q = start >> 7
                r = start & (LANES - 1)
                turn = (LANES - r) & (LANES - 1)
                keep = lane8 < LANES - r
                for part in range(2):
                    row = d * rows8 + part * p_dev + p
                    low = pltpu.roll(prof_ref[pl.ds(row * stride + q, pieces), :], turn, 1)
                    high = pltpu.roll(prof_ref[pl.ds(row * stride + q + 1, pieces), :], turn, 1)
                    at = row * (pieces + 1)
                    cut_ref[pl.ds(at + 1, pieces), :] = high
                    cut_ref[pl.ds(at, pieces), :] = jnp.where(keep, low, high)
            return carry

        n = n_dev // 2
        lax.fori_loop(part_of * n, (part_of + 1) * n, owner, 0, unroll=4)

    def pack(c, part_of):
        first = part_of * (rows // 2) * (pieces + 1) + c
        return cut_ref[pl.ds(first, rows // 2, stride=pieces + 1), :].astype(BF16)

    def band_move(part_of, to):
        here = pl.ds(part_of * (rows // 2), rows // 2)
        return pltpu.make_async_remote_copy(
            src_ref=out_buf.at[here], dst_ref=bands_ref.at[to, here],
            send_sem=p_send.at[part_of], recv_sem=p_recv.at[part_of],
            device_id=(me_p, partner), device_id_type=MESH,
        )

    band_moves = [band_move(part_of, core) for part_of in range(2)]
    for part_of in range(2):
        cut_bands(partner, part_of)
        here = slice(part_of * (rows // 2), (part_of + 1) * (rows // 2))
        for c in range(pieces + 1):
            out_buf[here, c * LANES : (c + 1) * LANES] = pack(c, part_of)
        band_moves[part_of].start()
    for part_of in range(2):
        cut_bands(me_t, part_of)
        here = slice(part_of * (rows // 2), (part_of + 1) * (rows // 2))
        for c in range(pieces + 1):
            bands_ref[core, here, c * LANES : (c + 1) * LANES] = pack(c, part_of)
    pltpu.make_async_remote_copy(
        src_ref=meta_ref.at[1 - core], dst_ref=meta_ref.at[1 - core],
        send_sem=p_send.at[2], recv_sem=p_recv.at[2],
        device_id=(me_p, partner), device_id_type=MESH,
    ).wait_recv()
    meta = meta_ref[...].reshape(2 * n_dev, meta_ref.shape[3]).astype(F32).astype(BF16)
    blk = spread(meta, 0, rows8, n_rows)
    fine = spread(meta, 1, rows8, n_rows) * (1.0 / 16.0)
    dop = spread(meta, 2, rows8, n_rows) + DOP_SPLIT * spread(meta, 3, rows8, n_rows)
    sel = lax.broadcasted_iota(jnp.int32, (2 * steps, n_rows), 0)
    col = lax.broadcasted_iota(jnp.int32, (2 * steps, n_rows), 1)
    in_block = (sel // 2).astype(F32) == blk
    same = in_block & (sel % 2 == (col % rows8) // p_dev)
    zero = jnp.zeros((2 * steps, n_rows), F32)
    left = jnp.concatenate([jnp.where(same, 1.0, zero), jnp.where(same, fine, zero)], 0).astype(BF16)
    for part_of in range(2):
        band_move(part_of, 1 - core).wait_recv()
    bands = bands_ref[...].reshape(n_rows, ext)
    ab = jnp.dot(left, bands, preferred_element_type=F32)
    k = 2 * steps
    a, b = ab[:k], ab[k:]
    pc = a - b + pltpu.roll(b, ext - 1, 1)
    qc = pltpu.roll(a, ext - 1, 1) - a
    inside = lax.broadcasted_iota(jnp.int32, pc.shape, 1) < band
    x = jnp.where(inside, 4.0 * pc + 1.5 * qc, 0.0)
    y = jnp.where(inside, 1.5 * pc + 0.875 * qc, 0.0)
    x0 = x - y + pltpu.roll(y, 1, 1)
    x1 = pltpu.roll(x, 1, 1) - x
    xs = jnp.concatenate(thirds(x0) + thirds(x1), 0)
    d6 = lax.dot_general(xs, bands, (((1,), (1,)), ((), ())), preferred_element_type=F32)
    d0 = d6[2 * k : 3 * k] + d6[k : 2 * k] + d6[:k]
    d1 = d6[5 * k : 6 * k] + d6[4 * k : 5 * k] + d6[3 * k : 4 * k]
    h = d0 + fine * d1
    hr = jnp.sum(jnp.where(in_block & (sel % 2 == 0), h, 0.0), axis=0, keepdims=True)
    hi = jnp.sum(jnp.where(in_block & (sel % 2 == 1), h, 0.0), axis=0, keepdims=True)
    both = jnp.concatenate([hr, hi, jnp.zeros((6, n_rows), F32)], 0)
    part1 = (lax.broadcasted_iota(jnp.int32, (8, n_rows), 1) % rows8) >= p_dev
    other = swap_parts(both, part1, p_dev)
    hr, hi, hr_o, hi_o = both[0:1], both[1:2], other[0:1], other[1:2]
    one = part1[0:1]
    g_ref[0:1] = jnp.where(one, hr_o + hi, hr + hi_o)
    g_ref[1:2] = jnp.where(one, hr - hi_o, hr_o - hi)
    g_moves = [
        pltpu.make_async_remote_copy(
            src_ref=g_ref, dst_ref=got_ref.at[d],
            send_sem=g_send.at[d], recv_sem=g_recv.at[d],
            device_id=any_tile(d), device_id_type=MESH,
        )
        for d in range(1, n_tile)
    ]
    for move in g_moves:
        move.start()
    total_rows = r_dev * n_pulse
    image_row = me_p * r_dev + lax.broadcasted_iota(jnp.int32, (r_dev, n_rows), 0)
    turns = dop.astype(jnp.int32) * image_row
    if total_rows & (total_rows - 1):
        turns = turns % total_rows
    else:
        turns = turns & (total_rows - 1)
    angle = 2.0 * jnp.pi * turns.astype(F32) / total_rows
    norm = 1.0 / jnp.sqrt(F32(n_rows // 2))
    er = (jnp.cos(angle) * norm).astype(BF16).astype(F32)
    ei = (jnp.sin(angle) * norm).astype(BF16).astype(F32)
    square = (n_rows, n_rows)
    diagonal = lax.broadcasted_iota(jnp.int32, square, 0) == lax.broadcasted_iota(jnp.int32, square, 1)
    fine_col = jnp.sum(jnp.where(diagonal, fine, 0.0), axis=1, keepdims=True)
    lane = lax.broadcasted_iota(jnp.int32, (n_rows, LANES), 1)
    for s in range(pieces):
        b0 = bands_ref[:, :, s * LANES : (s + 1) * LANES].reshape(n_rows, LANES).astype(F32)
        b1 = bands_ref[:, :, (s + 1) * LANES : (s + 2) * LANES].reshape(n_rows, LANES).astype(F32)
        b1 = pltpu.roll(jnp.where(lane == 0, b1, b0), LANES - 1, 1)
        bend = fine_col * (b1 - b0)
        pair = jnp.concatenate([b0 + bend, b1 + bend], 1).astype(BF16)
        samp_ref[:, 4 * s * LANES : 4 * (s + 1) * LANES] = jnp.dot(
            pair, up_ref[...], preferred_element_type=F32
        ).astype(BF16)
    total = g_ref[...]
    for d in range(1, n_tile):
        g_moves[d - 1].wait_recv()
        total = total + got_ref[d]
    g_re, g_im = total[0:1], total[1:2]
    scale = jnp.sqrt(g_re * g_re + g_im * g_im + 1.0)
    c_re = g_re / scale
    c_im = -g_im / scale
    alpha = jnp.where(one, -c_im, c_re)
    beta = jnp.where(one, c_re, c_im)
    w = (er * alpha - ei * beta, er * beta + ei * alpha)
    for z in range(2):
        here = pl.ds(z * r_dev, r_dev)
        left_ref[here, :] = w[z].astype(BF16)
    for c in started + [meta_move] + band_moves + g_moves:
        c.wait_send()


def focus(n_pulse, n_tile, r_dev, band, range_off, fine, dop, order, idx, raw, filt):
    p_dev = raw.shape[1]
    win, ups = filt.shape[1:]
    half = n_tile // 2
    n_dev = n_pulse * half
    rows = n_dev * 2 * p_dev
    n_rows = 2 * rows
    fields = 8 * p_dev + idx.size
    width = fields + -fields % LANES
    chunk = 2 * LANES
    sem = pltpu.SemaphoreType.DMA
    return pl.pallas_call(
        functools.partial(focus_kernel, n_pulse, n_tile, r_dev),
        out_shape=(
            pltpu.VMEM((2 * r_dev, n_rows), BF16),
            pltpu.VMEM((n_rows, 4 * band), BF16),
        ),
        in_specs=[pl.BlockSpec(memory_space=pltpu.HBM)] * 7,
        out_specs=[pl.BlockSpec(memory_space=pltpu.VMEM)] * 2,
        scratch_shapes=[
            *[pltpu.SMEM(a.shape, jnp.int32) for a in (range_off, fine, dop, order, idx)],
            pltpu.VMEM(raw.shape, BF16),
            pltpu.VMEM((2, rows, band + LANES), BF16),
            pltpu.VMEM((2 * LANES, 4 * LANES), BF16),
            pltpu.VMEM((n_dev, 2 * p_dev, win), BF16),
            pltpu.VMEM((2, n_dev, 1, width), jnp.int32),
            pltpu.SMEM((n_dev, 1, width), jnp.int32),
            pltpu.VMEM((ups // chunk, 2, win, chunk), BF16),
            pltpu.VMEM((2, rows, win), BF16),
            pltpu.VMEM((rows * (ups // LANES) + 8, LANES), F32),
            pltpu.VMEM((rows * (band // LANES + 1), LANES), F32),
            pltpu.VMEM((rows, band + LANES), BF16),
            pltpu.VMEM((2, n_rows), F32),
            pltpu.VMEM((n_tile, 2, n_rows), F32),
            sem((6,)),
            sem((ups // chunk,)),
            sem,
            sem((2, n_pulse)),
            sem((2, n_pulse)),
            sem((2, n_pulse, half)),
            sem((2, n_pulse, half)),
            sem((3,)),
            sem((3,)),
            sem((n_tile,)),
            sem((n_tile,)),
        ],
        compiler_params=pltpu.CompilerParams(
            collective_id=0, has_side_effects=True, vmem_limit_bytes=VMEM_LIMIT
        ),
    )(*[pltpu.with_memory_space_constraint(a, pltpu.HBM) for a in (range_off, fine, dop, order, idx, raw, filt)])


def image_kernel(left_ref, samp_ref, out_ref, res_ref, sem):
    r_dev = out_ref.shape[1]
    parts = sem.shape[0]
    width = out_ref.shape[2] // parts
    moves = []
    for i in range(parts):
        cols = pl.ds(i * width, width)
        res = jnp.dot(left_ref[...], samp_ref[:, cols], preferred_element_type=F32).astype(BF16)
        for z in range(2):
            res_ref[z, :, cols] = res[z * r_dev : (z + 1) * r_dev]
        move = pltpu.make_async_copy(res_ref.at[:, :, cols], out_ref.at[:, :, cols], sem.at[i])
        move.start()
        moves.append(move)
    for move in moves:
        move.wait()


def image(left, samples, r_dev):
    cols = samples.shape[1]
    return pl.pallas_call(
        image_kernel,
        out_shape=jax.ShapeDtypeStruct((2, r_dev, cols), BF16),
        in_specs=[pl.BlockSpec(memory_space=pltpu.VMEM)] * 2,
        out_specs=pl.BlockSpec(memory_space=pltpu.HBM),
        scratch_shapes=[pltpu.VMEM((2, r_dev, cols), BF16), pltpu.SemaphoreType.DMA((8,))],
        compiler_params=pltpu.CompilerParams(vmem_limit_bytes=IMAGE_VMEM),
    )(left, samples)


BAND = 1024
R_DEV = 128


def shards(raw, filt, range_off, fine, dop, pulse_order, band_idx):
    n_pulse = lax.axis_size("pulse")
    n_tile = lax.axis_size("tile")
    left, samples = focus(
        n_pulse, n_tile, R_DEV, BAND, range_off, fine, dop, pulse_order, band_idx.T, raw, filt
    )
    return image(left, samples, R_DEV)


def solution(mesh):
    return jax.shard_map(
        shards,
        mesh=mesh,
        in_specs=(
            P(None, ("pulse", "tile"), None),
            P(),
            P(("pulse", "tile")),
            P(("pulse", "tile")),
            P(("pulse", "tile")),
            P(("pulse", "tile"), None),
            P(None, ("pulse", "tile")),
        ),
        out_specs=P(None, "pulse", "tile"),
        check_vma=False,
    )
```

```python
import functools

import jax
import jax.numpy as jnp
from jax import lax
from jax.experimental import pallas as pl
from jax.experimental.pallas import tpu as pltpu
from jax.sharding import PartitionSpec as P

F32 = jnp.float32
BF16 = jnp.bfloat16
MESH = pl.DeviceIdType.MESH
LANES = 128
DOP_SPLIT = 32
VMEM_LIMIT = 44 * 1024 * 1024
IMAGE_VMEM = 16 * 1024 * 1024


def spread(meta, field, rows8, n_rows):
    lane = lax.broadcasted_iota(jnp.int32, (meta.shape[1], n_rows), 0)
    col = lax.broadcasted_iota(jnp.int32, (meta.shape[1], n_rows), 1)
    pick = (lane == field * rows8 + col % rows8).astype(F32).astype(BF16)
    wide = jnp.dot(meta, pick, preferred_element_type=F32)
    owner = lax.broadcasted_iota(jnp.int32, wide.shape, 0)
    column = lax.broadcasted_iota(jnp.int32, wide.shape, 1)
    return jnp.sum(jnp.where(owner == column // rows8, wide, 0.0), axis=0, keepdims=True)


def thirds(x):
    a = x.astype(BF16)
    rest = x - a.astype(F32)
    b = rest.astype(BF16)
    return [a, b, (rest - b.astype(F32)).astype(BF16)]


def swap_parts(v, part1, p_dev):
    n = v.shape[-1]
    return jnp.where(part1, pltpu.roll(v, p_dev, 1), pltpu.roll(v, n - p_dev, 1))


def focus_kernel(
    n_pulse, n_tile, r_dev,
    off_in, fine_in, dop_in, order_in, idx_in, raw_in, filt_ref,
    left_ref, samp_ref,
    off_ref, fine_ref, dop_ref, order_ref, idx_ref, raw_ref,
    bands_ref, up_ref, win_ref, meta_ref, scal_ref, filt_buf, x_ref, prof_ref, cut_ref, out_buf, g_ref, got_ref,
    past_sem, i_sem, f_sem, s_sem, z_send, z_recv, t_send, t_recv, p_send, p_recv, g_send, g_recv,
):
    me_p = lax.axis_index("pulse")
    me_t = lax.axis_index("tile")
    half = n_tile // 2
    core = me_t % 2
    chip = me_t // 2
    partner = chip * 2 + (1 - core)
    p_dev = raw_ref.shape[1]
    steps = order_ref.shape[1]
    raw_len = raw_ref.shape[2]
    win = x_ref.shape[2]
    rows = x_ref.shape[1]
    rows8 = 2 * p_dev
    n_dev = n_pulse * half
    n_rows = 2 * rows
    chunks, chunk = filt_buf.shape[0], filt_buf.shape[3]
    stride = prof_ref.shape[0] // rows
    ext = bands_ref.shape[2]
    band = ext - LANES
    pieces = band // LANES

    def pulse_at(i):
        low, high = me_p, n_pulse - 1 - me_p
        both = jnp.minimum(low, high)
        two_sided = i <= 2 * both
        dist = jnp.where(two_sided, (i + 1) // 2, i - both)
        up = jnp.where(two_sided, i % 2, jnp.where(high > low, 1, 0))
        return me_p + (2 * up - 1) * dist

    def pulse_peer(d):
        return (lax.rem(me_p + d, n_pulse), me_t)

    def flip(k):
        bits = [1 << n for n in range(half.bit_length() - 1)]
        return sum(((chip // b + k // b) % 2) * b for b in bits)

    def tile_peer(k):
        return (me_p, flip(k) * 2 + core)

    def any_tile(d):
        return (me_p, lax.rem(me_t + d, n_tile))

    barrier = pltpu.get_barrier_semaphore()
    for d in range(1, n_pulse):
        pl.semaphore_signal(barrier, 1, device_id=pulse_peer(d), device_id_type=MESH)
    near = [1, 2] if half == 4 else list(range(1, half))
    greeted = [tile_peer(k) for k in near] + [(me_p, partner)]
    if half != 4:
        greeted += [(me_p, flip(k) * 2 + 1 - core) for k in near]
    for peer in greeted:
        pl.semaphore_signal(barrier, 1, device_id=peer, device_id_type=MESH)

    def load_filter(n):
        return pltpu.make_async_copy(
            filt_ref.at[:, :, pl.ds(n * chunk, chunk)], filt_buf.at[n], f_sem.at[n]
        )

    inputs = [
        pltpu.make_async_copy(src, dst, i_sem.at[n])
        for n, (src, dst) in enumerate(
            [(raw_in, raw_ref), (off_in, off_ref), (order_in, order_ref)]
            + [(fine_in, fine_ref), (dop_in, dop_ref), (idx_in, idx_ref)]
        )
    ]
    for copy in inputs:
        copy.start()
    for copy in inputs:
        copy.wait()
    for n in range(chunks):
        load_filter(n).start()

    raw = jnp.concatenate([raw_ref[0].astype(F32), raw_ref[1].astype(F32)], 0)
    row = lax.broadcasted_iota(jnp.int32, (rows8, win), 0)
    cut = jnp.zeros((rows8, win), F32)
    for p in range(p_dev):
        off = off_ref[p]
        shift = jnp.where(off == 0, 0, raw_len - off)
        turned = pltpu.roll(raw, shift, 1)[:, :win]
        cut = jnp.where(row % p_dev == p, turned, cut)
    mine = me_p * half + chip
    win_ref[mine] = cut.astype(BF16)
    lane = lax.broadcasted_iota(jnp.int32, meta_ref.shape[2:], 1)
    line = jnp.zeros(meta_ref.shape[2:], jnp.int32)
    for p in range(p_dev):
        pulse_lane = (lane < 4 * rows8) & (lane % p_dev == p)
        line = jnp.where(pulse_lane & (lane // rows8 == 1), fine_ref[p], line)
        line = jnp.where(pulse_lane & (lane // rows8 == 2), dop_ref[p] % DOP_SPLIT, line)
        line = jnp.where(pulse_lane & (lane // rows8 == 3), dop_ref[p] // DOP_SPLIT, line)
        line = jnp.where((lane < rows8) & (lane % p_dev == order_ref[0, p]), p, line)
        for t in range(n_tile):
            line = jnp.where(lane == 4 * rows8 + t * p_dev + p, idx_ref[p, t], line)
    meta_ref[core, mine] = line
    j = lax.broadcasted_iota(jnp.int32, up_ref.shape, 0)
    c = lax.broadcasted_iota(jnp.int32, up_ref.shape, 1)
    w = (c % 4).astype(F32) * 0.25
    up = jnp.where(j < LANES, 1.0 - w, w)
    up_ref[...] = jnp.where(j % LANES == c // 4, up, 0.0).astype(BF16)
    pl.semaphore_wait(barrier, n_pulse - 1 + len(greeted))
    if half == 4:
        pl.semaphore_signal(past_sem, 1, device_id=tile_peer(1), device_id_type=MESH)

    def copies(slot, send, recv, at, target):
        return [
            pltpu.make_async_remote_copy(
                src_ref=ref, dst_ref=ref, send_sem=send.at[(a,) + at], recv_sem=recv.at[(a,) + at],
                device_id=target, device_id_type=MESH,
            )
            for a, ref in enumerate((win_ref.at[slot], meta_ref.at[core, slot]))
        ]

    started = []

    def send(*args):
        for c in copies(*args):
            c.start()
            started.append(c)

    def arrive(*args):
        for c in copies(*args):
            c.wait_recv()

    nearest = [pulse_at(i) for i in range(1, n_pulse)]
    for q in reversed(nearest):
        d = lax.rem(q - me_p + n_pulse, n_pulse)
        send(mine, z_send, z_recv, (d,), (q, me_t))
    for q in [me_p] + nearest:
        dp = lax.rem(me_p - q + n_pulse, n_pulse)
        slot = q * half + chip
        if q is not me_p:
            arrive(slot, z_send, z_recv, (dp,), (q, me_t))
        else:
            for k in near:
                send(slot, t_send, t_recv, (dp, k), tile_peer(k))
            if half == 4:
                pl.semaphore_wait(past_sem, 1)
        for k in reversed(range(1, half)):
            if q is not me_p or k not in near:
                send(slot, t_send, t_recv, (dp, k), tile_peer(k))
    for q in [me_p] + nearest:
        dp = lax.rem(me_p - q + n_pulse, n_pulse)
        for k in range(1, half):
            arrive(q * half + flip(k), t_send, t_recv, (dp, k), tile_peer(k))

    to_scalar = pltpu.make_async_copy(meta_ref.at[core], scal_ref, s_sem)
    to_scalar.start()
    meta_move = pltpu.make_async_remote_copy(
        src_ref=meta_ref.at[core], dst_ref=meta_ref.at[core],
        send_sem=p_send.at[2], recv_sem=p_recv.at[2],
        device_id=(me_p, partner), device_id_type=MESH,
    )
    meta_move.start()
    for n in range(chunks):
        load_filter(n).wait()
    x = win_ref[...].astype(F32)
    r = lax.broadcasted_iota(jnp.int32, x.shape, 1)
    y = jnp.where(r < p_dev, -1.0, 1.0) * pltpu.roll(x, p_dev, 1)
    x_ref[0] = x.reshape(rows, win).astype(BF16)
    x_ref[1] = y.reshape(rows, win).astype(BF16)

    for n in range(chunks):
        acc = jnp.dot(x_ref[0], filt_buf[n, 0], preferred_element_type=F32) + jnp.dot(
            x_ref[1], filt_buf[n, 1], preferred_element_type=F32
        )
        for c in range(chunk // LANES):
            prof_ref[pl.ds(n * (chunk // LANES) + c, rows, stride=stride), :] = acc[
                :, c * LANES : (c + 1) * LANES
            ]
    to_scalar.wait()
    lane8 = lax.broadcasted_iota(jnp.int32, (pieces, LANES), 1)

    def cut_bands(tile, part_of):
        def owner(d, carry):
            for p in range(p_dev):
                start = scal_ref[d, 0, 4 * rows8 + tile * p_dev + p]
                q = start >> 7
                r = start & (LANES - 1)
                turn = (LANES - r) & (LANES - 1)
                keep = lane8 < LANES - r
                for part in range(2):
                    row = d * rows8 + part * p_dev + p
                    low = pltpu.roll(prof_ref[pl.ds(row * stride + q, pieces), :], turn, 1)
                    high = pltpu.roll(prof_ref[pl.ds(row * stride + q + 1, pieces), :], turn, 1)
                    at = row * (pieces + 1)
                    cut_ref[pl.ds(at + 1, pieces), :] = high
                    cut_ref[pl.ds(at, pieces), :] = jnp.where(keep, low, high)
            return carry

        n = n_dev // 2
        lax.fori_loop(part_of * n, (part_of + 1) * n, owner, 0, unroll=4)

    def pack(c, part_of):
        first = part_of * (rows // 2) * (pieces + 1) + c
        return cut_ref[pl.ds(first, rows // 2, stride=pieces + 1), :].astype(BF16)

    def band_move(part_of, to):
        here = pl.ds(part_of * (rows // 2), rows // 2)
        return pltpu.make_async_remote_copy(
            src_ref=out_buf.at[here], dst_ref=bands_ref.at[to, here],
            send_sem=p_send.at[part_of], recv_sem=p_recv.at[part_of],
            device_id=(me_p, partner), device_id_type=MESH,
        )

    band_moves = [band_move(part_of, core) for part_of in range(2)]
    for part_of in range(2):
        cut_bands(partner, part_of)
        here = slice(part_of * (rows // 2), (part_of + 1) * (rows // 2))
        for c in range(pieces + 1):
            out_buf[here, c * LANES : (c + 1) * LANES] = pack(c, part_of)
        band_moves[part_of].start()
    for part_of in range(2):
        cut_bands(me_t, part_of)
        here = slice(part_of * (rows // 2), (part_of + 1) * (rows // 2))
        for c in range(pieces + 1):
            bands_ref[core, here, c * LANES : (c + 1) * LANES] = pack(c, part_of)
    pltpu.make_async_remote_copy(
        src_ref=meta_ref.at[1 - core], dst_ref=meta_ref.at[1 - core],
        send_sem=p_send.at[2], recv_sem=p_recv.at[2],
        device_id=(me_p, partner), device_id_type=MESH,
    ).wait_recv()
    meta = meta_ref[...].reshape(2 * n_dev, meta_ref.shape[3]).astype(F32).astype(BF16)
    blk = spread(meta, 0, rows8, n_rows)
    fine = spread(meta, 1, rows8, n_rows) * (1.0 / 16.0)
    dop = spread(meta, 2, rows8, n_rows) + DOP_SPLIT * spread(meta, 3, rows8, n_rows)
    sel = lax.broadcasted_iota(jnp.int32, (2 * steps, n_rows), 0)
    col = lax.broadcasted_iota(jnp.int32, (2 * steps, n_rows), 1)
    in_block = (sel // 2).astype(F32) == blk
    same = in_block & (sel % 2 == (col % rows8) // p_dev)
    zero = jnp.zeros((2 * steps, n_rows), F32)
    left = jnp.concatenate([jnp.where(same, 1.0, zero), jnp.where(same, fine, zero)], 0).astype(BF16)
    for part_of in range(2):
        band_move(part_of, 1 - core).wait_recv()
    bands = bands_ref[...].reshape(n_rows, ext)
    ab = jnp.dot(left, bands, preferred_element_type=F32)
    k = 2 * steps
    a, b = ab[:k], ab[k:]
    pc = a - b + pltpu.roll(b, ext - 1, 1)
    qc = pltpu.roll(a, ext - 1, 1) - a
    inside = lax.broadcasted_iota(jnp.int32, pc.shape, 1) < band
    x = jnp.where(inside, 4.0 * pc + 1.5 * qc, 0.0)
    y = jnp.where(inside, 1.5 * pc + 0.875 * qc, 0.0)
    x0 = x - y + pltpu.roll(y, 1, 1)
    x1 = pltpu.roll(x, 1, 1) - x
    xs = jnp.concatenate(thirds(x0) + thirds(x1), 0)
    d6 = lax.dot_general(xs, bands, (((1,), (1,)), ((), ())), preferred_element_type=F32)
    d0 = d6[2 * k : 3 * k] + d6[k : 2 * k] + d6[:k]
    d1 = d6[5 * k : 6 * k] + d6[4 * k : 5 * k] + d6[3 * k : 4 * k]
    h = d0 + fine * d1
    hr = jnp.sum(jnp.where(in_block & (sel % 2 == 0), h, 0.0), axis=0, keepdims=True)
    hi = jnp.sum(jnp.where(in_block & (sel % 2 == 1), h, 0.0), axis=0, keepdims=True)
    both = jnp.concatenate([hr, hi, jnp.zeros((6, n_rows), F32)], 0)
    part1 = (lax.broadcasted_iota(jnp.int32, (8, n_rows), 1) % rows8) >= p_dev
    other = swap_parts(both, part1, p_dev)
    hr, hi, hr_o, hi_o = both[0:1], both[1:2], other[0:1], other[1:2]
    one = part1[0:1]
    g_ref[0:1] = jnp.where(one, hr_o + hi, hr + hi_o)
    g_ref[1:2] = jnp.where(one, hr - hi_o, hr_o - hi)
    g_moves = [
        pltpu.make_async_remote_copy(
            src_ref=g_ref, dst_ref=got_ref.at[d],
            send_sem=g_send.at[d], recv_sem=g_recv.at[d],
            device_id=any_tile(d), device_id_type=MESH,
        )
        for d in range(1, n_tile)
    ]
    for move in g_moves:
        move.start()
    total_rows = r_dev * n_pulse
    image_row = me_p * r_dev + lax.broadcasted_iota(jnp.int32, (r_dev, n_rows), 0)
    turns = dop.astype(jnp.int32) * image_row
    if total_rows & (total_rows - 1):
        turns = turns % total_rows
    else:
        turns = turns & (total_rows - 1)
    angle = 2.0 * jnp.pi * turns.astype(F32) / total_rows
    norm = 1.0 / jnp.sqrt(F32(n_rows // 2))
    er = (jnp.cos(angle) * norm).astype(BF16).astype(F32)
    ei = (jnp.sin(angle) * norm).astype(BF16).astype(F32)
    square = (n_rows, n_rows)
    diagonal = lax.broadcasted_iota(jnp.int32, square, 0) == lax.broadcasted_iota(jnp.int32, square, 1)
    fine_col = jnp.sum(jnp.where(diagonal, fine, 0.0), axis=1, keepdims=True)
    lane = lax.broadcasted_iota(jnp.int32, (n_rows, LANES), 1)
    for s in range(pieces):
        b0 = bands_ref[:, :, s * LANES : (s + 1) * LANES].reshape(n_rows, LANES).astype(F32)
        b1 = bands_ref[:, :, (s + 1) * LANES : (s + 2) * LANES].reshape(n_rows, LANES).astype(F32)
        b1 = pltpu.roll(jnp.where(lane == 0, b1, b0), LANES - 1, 1)
        bend = fine_col * (b1 - b0)
        pair = jnp.concatenate([b0 + bend, b1 + bend], 1).astype(BF16)
        samp_ref[:, 4 * s * LANES : 4 * (s + 1) * LANES] = jnp.dot(
            pair, up_ref[...], preferred_element_type=F32
        ).astype(BF16)
    total = g_ref[...]
    for d in range(1, n_tile):
        g_moves[d - 1].wait_recv()
        total = total + got_ref[d]
    g_re, g_im = total[0:1], total[1:2]
    scale = jnp.sqrt(g_re * g_re + g_im * g_im + 1.0)
    c_re = g_re / scale
    c_im = -g_im / scale
    alpha = jnp.where(one, -c_im, c_re)
    beta = jnp.where(one, c_re, c_im)
    w = (er * alpha - ei * beta, er * beta + ei * alpha)
    for z in range(2):
        here = pl.ds(z * r_dev, r_dev)
        left_ref[here, :] = w[z].astype(BF16)
    for c in started + [meta_move] + band_moves + g_moves:
        c.wait_send()


def focus(n_pulse, n_tile, r_dev, band, range_off, fine, dop, order, idx, raw, filt):
    p_dev = raw.shape[1]
    win, ups = filt.shape[1:]
    half = n_tile // 2
    n_dev = n_pulse * half
    rows = n_dev * 2 * p_dev
    n_rows = 2 * rows
    fields = 8 * p_dev + idx.size
    width = fields + -fields % LANES
    chunk = 2 * LANES
    sem = pltpu.SemaphoreType.DMA
    return pl.pallas_call(
        functools.partial(focus_kernel, n_pulse, n_tile, r_dev),
        out_shape=(
            pltpu.VMEM((2 * r_dev, n_rows), BF16),
            pltpu.VMEM((n_rows, 4 * band), BF16),
        ),
        in_specs=[pl.BlockSpec(memory_space=pltpu.HBM)] * 7,
        out_specs=[pl.BlockSpec(memory_space=pltpu.VMEM)] * 2,
        scratch_shapes=[
            *[pltpu.SMEM(a.shape, jnp.int32) for a in (range_off, fine, dop, order, idx)],
            pltpu.VMEM(raw.shape, BF16),
            pltpu.VMEM((2, rows, band + LANES), BF16),
            pltpu.VMEM((2 * LANES, 4 * LANES), BF16),
            pltpu.VMEM((n_dev, 2 * p_dev, win), BF16),
            pltpu.VMEM((2, n_dev, 1, width), jnp.int32),
            pltpu.SMEM((n_dev, 1, width), jnp.int32),
            pltpu.VMEM((ups // chunk, 2, win, chunk), BF16),
            pltpu.VMEM((2, rows, win), BF16),
            pltpu.VMEM((rows * (ups // LANES) + 8, LANES), F32),
            pltpu.VMEM((rows * (band // LANES + 1), LANES), F32),
            pltpu.VMEM((rows, band + LANES), BF16),
            pltpu.VMEM((2, n_rows), F32),
            pltpu.VMEM((n_tile, 2, n_rows), F32),
            pltpu.SemaphoreType.REGULAR,
            sem((6,)),
            sem((ups // chunk,)),
            sem,
            sem((2, n_pulse)),
            sem((2, n_pulse)),
            sem((2, n_pulse, half)),
            sem((2, n_pulse, half)),
            sem((3,)),
            sem((3,)),
            sem((n_tile,)),
            sem((n_tile,)),
        ],
        compiler_params=pltpu.CompilerParams(
            collective_id=0, has_side_effects=True, vmem_limit_bytes=VMEM_LIMIT
        ),
    )(*[pltpu.with_memory_space_constraint(a, pltpu.HBM) for a in (range_off, fine, dop, order, idx, raw, filt)])


def image_kernel(left_ref, samp_ref, out_ref, res_ref, sem):
    r_dev = out_ref.shape[1]
    parts = sem.shape[0]
    width = out_ref.shape[2] // parts
    moves = []
    for i in range(parts):
        cols = pl.ds(i * width, width)
        res = jnp.dot(left_ref[...], samp_ref[:, cols], preferred_element_type=F32).astype(BF16)
        for z in range(2):
            res_ref[z, :, cols] = res[z * r_dev : (z + 1) * r_dev]
        move = pltpu.make_async_copy(res_ref.at[:, :, cols], out_ref.at[:, :, cols], sem.at[i])
        move.start()
        moves.append(move)
    for move in moves:
        move.wait()


def image(left, samples, r_dev):
    cols = samples.shape[1]
    return pl.pallas_call(
        image_kernel,
        out_shape=jax.ShapeDtypeStruct((2, r_dev, cols), BF16),
        in_specs=[pl.BlockSpec(memory_space=pltpu.VMEM)] * 2,
        out_specs=pl.BlockSpec(memory_space=pltpu.HBM),
        scratch_shapes=[pltpu.VMEM((2, r_dev, cols), BF16), pltpu.SemaphoreType.DMA((8,))],
        compiler_params=pltpu.CompilerParams(vmem_limit_bytes=IMAGE_VMEM),
    )(left, samples)


BAND = 1024
R_DEV = 128


def shards(raw, filt, range_off, fine, dop, pulse_order, band_idx):
    n_pulse = lax.axis_size("pulse")
    n_tile = lax.axis_size("tile")
    left, samples = focus(
        n_pulse, n_tile, R_DEV, BAND, range_off, fine, dop, pulse_order, band_idx.T, raw, filt
    )
    return image(left, samples, R_DEV)


def solution(mesh):
    return jax.shard_map(
        shards,
        mesh=mesh,
        in_specs=(
            P(None, ("pulse", "tile"), None),
            P(),
            P(("pulse", "tile")),
            P(("pulse", "tile")),
            P(("pulse", "tile")),
            P(("pulse", "tile"), None),
            P(None, ("pulse", "tile")),
        ),
        out_specs=P(None, "pulse", "tile"),
        check_vma=False,
    )
```

```python
import functools

import jax
import jax.numpy as jnp
from jax import lax
from jax.experimental import pallas as pl
from jax.experimental.pallas import tpu as pltpu
from jax.sharding import PartitionSpec as P

F32 = jnp.float32
BF16 = jnp.bfloat16
MESH = pl.DeviceIdType.MESH
LANES = 128
DOP_SPLIT = 32
VMEM_LIMIT = 44 * 1024 * 1024
IMAGE_VMEM = 16 * 1024 * 1024


def spread(meta, field, rows8, n_rows):
    lane = lax.broadcasted_iota(jnp.int32, (meta.shape[1], n_rows), 0)
    col = lax.broadcasted_iota(jnp.int32, (meta.shape[1], n_rows), 1)
    pick = (lane == field * rows8 + col % rows8).astype(F32).astype(BF16)
    wide = jnp.dot(meta, pick, preferred_element_type=F32)
    owner = lax.broadcasted_iota(jnp.int32, wide.shape, 0)
    column = lax.broadcasted_iota(jnp.int32, wide.shape, 1)
    return jnp.sum(jnp.where(owner == column // rows8, wide, 0.0), axis=0, keepdims=True)


def thirds(x):
    a = x.astype(BF16)
    rest = x - a.astype(F32)
    b = rest.astype(BF16)
    return [a, b, (rest - b.astype(F32)).astype(BF16)]


def swap_parts(v, part1, p_dev):
    n = v.shape[-1]
    return jnp.where(part1, pltpu.roll(v, p_dev, 1), pltpu.roll(v, n - p_dev, 1))


def focus_kernel(
    n_pulse, n_tile, r_dev,
    off_in, fine_in, dop_in, order_in, idx_in, raw_in, filt_ref,
    left_ref, samp_ref,
    off_ref, fine_ref, dop_ref, order_ref, idx_ref, raw_ref,
    bands_ref, up_ref, win_ref, meta_ref, scal_ref, filt_buf, x_ref, prof_ref, cut_ref, out_buf, g_ref, got_ref,
    past_sem, i_sem, f_sem, s_sem, w_send, z_recv, t_recv, p_send, p_recv, g_send, g_recv,
):
    me_p = lax.axis_index("pulse")
    me_t = lax.axis_index("tile")
    half = n_tile // 2
    core = me_t % 2
    chip = me_t // 2
    partner = chip * 2 + (1 - core)
    p_dev = raw_ref.shape[1]
    steps = order_ref.shape[1]
    raw_len = raw_ref.shape[2]
    win = x_ref.shape[2]
    rows = x_ref.shape[1]
    rows8 = 2 * p_dev
    n_dev = n_pulse * half
    n_rows = 2 * rows
    chunk = 2 * LANES
    chunks = filt_buf.shape[2] // chunk
    stride = prof_ref.shape[0] // rows
    ext = bands_ref.shape[2]
    band = ext - LANES
    pieces = band // LANES

    def pulse_at(i):
        low, high = me_p, n_pulse - 1 - me_p
        both = jnp.minimum(low, high)
        two_sided = i <= 2 * both
        dist = jnp.where(two_sided, (i + 1) // 2, i - both)
        up = jnp.where(two_sided, i % 2, jnp.where(high > low, 1, 0))
        return me_p + (2 * up - 1) * dist

    def pulse_peer(d):
        return (lax.rem(me_p + d, n_pulse), me_t)

    def flip(k):
        bits = [1 << n for n in range(half.bit_length() - 1)]
        return sum(((chip // b + k // b) % 2) * b for b in bits)

    def tile_peer(k):
        return (me_p, flip(k) * 2 + core)

    def any_tile(d):
        return (me_p, lax.rem(me_t + d, n_tile))

    barrier = pltpu.get_barrier_semaphore()
    for d in range(1, n_pulse):
        pl.semaphore_signal(barrier, 1, device_id=pulse_peer(d), device_id_type=MESH)
    near = [1, 2] if half == 4 else list(range(1, half))
    greeted = [tile_peer(k) for k in near] + [(me_p, partner)]
    if half != 4:
        greeted += [(me_p, flip(k) * 2 + 1 - core) for k in near]
    for peer in greeted:
        pl.semaphore_signal(barrier, 1, device_id=peer, device_id_type=MESH)

    load_filter = pltpu.make_async_copy(filt_ref, filt_buf, f_sem)
    inputs = [
        pltpu.make_async_copy(src, dst, i_sem.at[n])
        for n, (src, dst) in enumerate(
            [(raw_in, raw_ref), (off_in, off_ref), (order_in, order_ref)]
            + [(fine_in, fine_ref), (dop_in, dop_ref), (idx_in, idx_ref)]
        )
    ]
    for copy in inputs:
        copy.start()
    for copy in inputs:
        copy.wait()
    load_filter.start()

    raw = jnp.concatenate([raw_ref[0].astype(F32), raw_ref[1].astype(F32)], 0)
    row = lax.broadcasted_iota(jnp.int32, (rows8, win), 0)
    cut = jnp.zeros((rows8, win), F32)
    for p in range(p_dev):
        off = off_ref[p]
        shift = jnp.where(off == 0, 0, raw_len - off)
        turned = pltpu.roll(raw, shift, 1)[:, :win]
        cut = jnp.where(row % p_dev == p, turned, cut)
    mine = me_p * half + chip
    win_ref[mine] = cut.astype(BF16)
    lane = lax.broadcasted_iota(jnp.int32, meta_ref.shape[2:], 1)
    line = jnp.zeros(meta_ref.shape[2:], jnp.int32)
    for p in range(p_dev):
        pulse_lane = (lane < 4 * rows8) & (lane % p_dev == p)
        line = jnp.where(pulse_lane & (lane // rows8 == 1), fine_ref[p], line)
        line = jnp.where(pulse_lane & (lane // rows8 == 2), dop_ref[p] % DOP_SPLIT, line)
        line = jnp.where(pulse_lane & (lane // rows8 == 3), dop_ref[p] // DOP_SPLIT, line)
        line = jnp.where((lane < rows8) & (lane % p_dev == order_ref[0, p]), p, line)
        for t in range(n_tile):
            line = jnp.where(lane == 4 * rows8 + t * p_dev + p, idx_ref[p, t], line)
    meta_ref[core, mine] = line
    j = lax.broadcasted_iota(jnp.int32, up_ref.shape, 0)
    c = lax.broadcasted_iota(jnp.int32, up_ref.shape, 1)
    w = (c % 4).astype(F32) * 0.25
    up = jnp.where(j < LANES, 1.0 - w, w)
    up_ref[...] = jnp.where(j % LANES == c // 4, up, 0.0).astype(BF16)
    pl.semaphore_wait(barrier, n_pulse - 1 + len(greeted))
    if half == 4:
        pl.semaphore_signal(past_sem, 1, device_id=tile_peer(1), device_id_type=MESH)

    def copies(slot, recv, at, target):
        return [
            pltpu.make_async_remote_copy(
                src_ref=ref, dst_ref=ref, send_sem=w_send.at[a], recv_sem=recv.at[(a,) + at],
                device_id=target, device_id_type=MESH,
            )
            for a, ref in enumerate((win_ref.at[slot], meta_ref.at[core, slot]))
        ]

    def send(*args):
        for c in copies(*args):
            c.start()

    def arrive(*args):
        for c in copies(*args):
            c.wait_recv()

    nearest = [pulse_at(i) for i in range(1, n_pulse)]
    for q in reversed(nearest):
        d = lax.rem(q - me_p + n_pulse, n_pulse)
        send(mine, z_recv, (d,), (q, me_t))
    for q in [me_p] + nearest:
        dp = lax.rem(me_p - q + n_pulse, n_pulse)
        slot = q * half + chip
        if q is not me_p:
            arrive(slot, z_recv, (dp,), (q, me_t))
        else:
            for k in near:
                send(slot, t_recv, (), tile_peer(k))
            if half == 4:
                pl.semaphore_wait(past_sem, 1)
        for k in reversed(range(1, half)):
            if q is not me_p or k not in near:
                send(slot, t_recv, (), tile_peer(k))
    arrive(pl.ds(0, n_pulse * (half - 1)), t_recv, (), tile_peer(1))

    to_scalar = pltpu.make_async_copy(meta_ref.at[core], scal_ref, s_sem)
    to_scalar.start()
    meta_move = pltpu.make_async_remote_copy(
        src_ref=meta_ref.at[core], dst_ref=meta_ref.at[core],
        send_sem=p_send.at[2], recv_sem=p_recv.at[2],
        device_id=(me_p, partner), device_id_type=MESH,
    )
    meta_move.start()
    load_filter.wait()
    x = win_ref[...].astype(F32)
    r = lax.broadcasted_iota(jnp.int32, x.shape, 1)
    y = jnp.where(r < p_dev, -1.0, 1.0) * pltpu.roll(x, p_dev, 1)
    x_ref[0] = x.reshape(rows, win).astype(BF16)
    x_ref[1] = y.reshape(rows, win).astype(BF16)

    for n in range(chunks):
        cols = slice(n * chunk, (n + 1) * chunk)
        acc = jnp.dot(x_ref[0], filt_buf[0, :, cols], preferred_element_type=F32) + jnp.dot(
            x_ref[1], filt_buf[1, :, cols], preferred_element_type=F32
        )
        for c in range(chunk // LANES):
            prof_ref[pl.ds(n * (chunk // LANES) + c, rows, stride=stride), :] = acc[
                :, c * LANES : (c + 1) * LANES
            ]
    to_scalar.wait()
    lane8 = lax.broadcasted_iota(jnp.int32, (pieces, LANES), 1)

    def cut_bands(tile, part_of):
        def owner(d, carry):
            for p in range(p_dev):
                start = scal_ref[d, 0, 4 * rows8 + tile * p_dev + p]
                q = start >> 7
                r = start & (LANES - 1)
                turn = (LANES - r) & (LANES - 1)
                keep = lane8 < LANES - r
                for part in range(2):
                    row = d * rows8 + part * p_dev + p
                    low = pltpu.roll(prof_ref[pl.ds(row * stride + q, pieces), :], turn, 1)
                    high = pltpu.roll(prof_ref[pl.ds(row * stride + q + 1, pieces), :], turn, 1)
                    at = row * (pieces + 1)
                    cut_ref[pl.ds(at + 1, pieces), :] = high
                    cut_ref[pl.ds(at, pieces), :] = jnp.where(keep, low, high)
            return carry

        n = n_dev // 2
        lax.fori_loop(part_of * n, (part_of + 1) * n, owner, 0, unroll=4)

    def pack(c, part_of):
        first = part_of * (rows // 2) * (pieces + 1) + c
        return cut_ref[pl.ds(first, rows // 2, stride=pieces + 1), :].astype(BF16)

    def band_move(part_of, to):
        here = pl.ds(part_of * (rows // 2), rows // 2)
        return pltpu.make_async_remote_copy(
            src_ref=out_buf.at[here], dst_ref=bands_ref.at[to, here],
            send_sem=p_send.at[part_of], recv_sem=p_recv.at[part_of],
            device_id=(me_p, partner), device_id_type=MESH,
        )

    band_moves = [band_move(part_of, core) for part_of in range(2)]
    for part_of in range(2):
        cut_bands(partner, part_of)
        here = slice(part_of * (rows // 2), (part_of + 1) * (rows // 2))
        for c in range(pieces + 1):
            out_buf[here, c * LANES : (c + 1) * LANES] = pack(c, part_of)
        band_moves[part_of].start()
    for part_of in range(2):
        cut_bands(me_t, part_of)
        here = slice(part_of * (rows // 2), (part_of + 1) * (rows // 2))
        for c in range(pieces + 1):
            bands_ref[core, here, c * LANES : (c + 1) * LANES] = pack(c, part_of)
    pltpu.make_async_remote_copy(
        src_ref=meta_ref.at[1 - core], dst_ref=meta_ref.at[1 - core],
        send_sem=p_send.at[2], recv_sem=p_recv.at[2],
        device_id=(me_p, partner), device_id_type=MESH,
    ).wait_recv()
    meta = meta_ref[...].reshape(2 * n_dev, meta_ref.shape[3]).astype(F32).astype(BF16)
    blk = spread(meta, 0, rows8, n_rows)
    fine = spread(meta, 1, rows8, n_rows) * (1.0 / 16.0)
    dop = spread(meta, 2, rows8, n_rows) + DOP_SPLIT * spread(meta, 3, rows8, n_rows)
    sel = lax.broadcasted_iota(jnp.int32, (2 * steps, n_rows), 0)
    col = lax.broadcasted_iota(jnp.int32, (2 * steps, n_rows), 1)
    in_block = (sel // 2).astype(F32) == blk
    same = in_block & (sel % 2 == (col % rows8) // p_dev)
    zero = jnp.zeros((2 * steps, n_rows), F32)
    left = jnp.concatenate([jnp.where(same, 1.0, zero), jnp.where(same, fine, zero)], 0).astype(BF16)
    for part_of in range(2):
        band_move(part_of, 1 - core).wait_recv()
    bands = bands_ref[...].reshape(n_rows, ext)
    ab = jnp.dot(left, bands, preferred_element_type=F32)
    k = 2 * steps
    a, b = ab[:k], ab[k:]
    pc = a - b + pltpu.roll(b, ext - 1, 1)
    qc = pltpu.roll(a, ext - 1, 1) - a
    inside = lax.broadcasted_iota(jnp.int32, pc.shape, 1) < band
    x = jnp.where(inside, 4.0 * pc + 1.5 * qc, 0.0)
    y = jnp.where(inside, 1.5 * pc + 0.875 * qc, 0.0)
    x0 = x - y + pltpu.roll(y, 1, 1)
    x1 = pltpu.roll(x, 1, 1) - x
    xs = jnp.concatenate(thirds(x0) + thirds(x1), 0)
    d6 = lax.dot_general(xs, bands, (((1,), (1,)), ((), ())), preferred_element_type=F32)
    d0 = d6[2 * k : 3 * k] + d6[k : 2 * k] + d6[:k]
    d1 = d6[5 * k : 6 * k] + d6[4 * k : 5 * k] + d6[3 * k : 4 * k]
    h = d0 + fine * d1
    hr = jnp.sum(jnp.where(in_block & (sel % 2 == 0), h, 0.0), axis=0, keepdims=True)
    hi = jnp.sum(jnp.where(in_block & (sel % 2 == 1), h, 0.0), axis=0, keepdims=True)
    both = jnp.concatenate([hr, hi, jnp.zeros((6, n_rows), F32)], 0)
    part1 = (lax.broadcasted_iota(jnp.int32, (8, n_rows), 1) % rows8) >= p_dev
    other = swap_parts(both, part1, p_dev)
    hr, hi, hr_o, hi_o = both[0:1], both[1:2], other[0:1], other[1:2]
    one = part1[0:1]
    g_ref[0:1] = jnp.where(one, hr_o + hi, hr + hi_o)
    g_ref[1:2] = jnp.where(one, hr - hi_o, hr_o - hi)
    g_moves = [
        pltpu.make_async_remote_copy(
            src_ref=g_ref, dst_ref=got_ref.at[d],
            send_sem=g_send, recv_sem=g_recv,
            device_id=any_tile(d), device_id_type=MESH,
        )
        for d in range(1, n_tile)
    ]
    for move in g_moves:
        move.start()
    total_rows = r_dev * n_pulse
    image_row = me_p * r_dev + lax.broadcasted_iota(jnp.int32, (r_dev, n_rows), 0)
    turns = dop.astype(jnp.int32) * image_row
    if total_rows & (total_rows - 1):
        turns = turns % total_rows
    else:
        turns = turns & (total_rows - 1)
    angle = 2.0 * jnp.pi * turns.astype(F32) / total_rows
    norm = 1.0 / jnp.sqrt(F32(n_rows // 2))
    er = (jnp.cos(angle) * norm).astype(BF16).astype(F32)
    ei = (jnp.sin(angle) * norm).astype(BF16).astype(F32)
    square = (n_rows, n_rows)
    diagonal = lax.broadcasted_iota(jnp.int32, square, 0) == lax.broadcasted_iota(jnp.int32, square, 1)
    fine_col = jnp.sum(jnp.where(diagonal, fine, 0.0), axis=1, keepdims=True)
    lane = lax.broadcasted_iota(jnp.int32, (n_rows, LANES), 1)
    for s in range(pieces):
        b0 = bands_ref[:, :, s * LANES : (s + 1) * LANES].reshape(n_rows, LANES).astype(F32)
        b1 = bands_ref[:, :, (s + 1) * LANES : (s + 2) * LANES].reshape(n_rows, LANES).astype(F32)
        b1 = pltpu.roll(jnp.where(lane == 0, b1, b0), LANES - 1, 1)
        bend = fine_col * (b1 - b0)
        pair = jnp.concatenate([b0 + bend, b1 + bend], 1).astype(BF16)
        samp_ref[:, 4 * s * LANES : 4 * (s + 1) * LANES] = jnp.dot(
            pair, up_ref[...], preferred_element_type=F32
        ).astype(BF16)
    total = g_ref[...]
    got_all = got_ref.at[pl.ds(1, n_tile - 1)]
    g_all = pltpu.make_async_remote_copy(
        src_ref=got_all, dst_ref=got_all, send_sem=g_send, recv_sem=g_recv,
        device_id=any_tile(1), device_id_type=MESH,
    )
    g_all.wait_recv()
    for d in range(1, n_tile):
        total = total + got_ref[d]
    g_re, g_im = total[0:1], total[1:2]
    scale = jnp.sqrt(g_re * g_re + g_im * g_im + 1.0)
    c_re = g_re / scale
    c_im = -g_im / scale
    alpha = jnp.where(one, -c_im, c_re)
    beta = jnp.where(one, c_re, c_im)
    w = (er * alpha - ei * beta, er * beta + ei * alpha)
    for z in range(2):
        here = pl.ds(z * r_dev, r_dev)
        left_ref[here, :] = w[z].astype(BF16)
    for c in copies(pl.ds(0, n_dev - 1), t_recv, (), tile_peer(1)) + [meta_move, g_all] + band_moves:
        c.wait_send()


def focus(n_pulse, n_tile, r_dev, band, range_off, fine, dop, order, idx, raw, filt):
    p_dev = raw.shape[1]
    win, ups = filt.shape[1:]
    half = n_tile // 2
    n_dev = n_pulse * half
    rows = n_dev * 2 * p_dev
    n_rows = 2 * rows
    fields = 8 * p_dev + idx.size
    width = fields + -fields % LANES
    sem = pltpu.SemaphoreType.DMA
    return pl.pallas_call(
        functools.partial(focus_kernel, n_pulse, n_tile, r_dev),
        out_shape=(
            pltpu.VMEM((2 * r_dev, n_rows), BF16),
            pltpu.VMEM((n_rows, 4 * band), BF16),
        ),
        in_specs=[pl.BlockSpec(memory_space=pltpu.HBM)] * 7,
        out_specs=[pl.BlockSpec(memory_space=pltpu.VMEM)] * 2,
        scratch_shapes=[
            *[pltpu.SMEM(a.shape, jnp.int32) for a in (range_off, fine, dop, order, idx)],
            pltpu.VMEM(raw.shape, BF16),
            pltpu.VMEM((2, rows, band + LANES), BF16),
            pltpu.VMEM((2 * LANES, 4 * LANES), BF16),
            pltpu.VMEM((n_dev, 2 * p_dev, win), BF16),
            pltpu.VMEM((2, n_dev, 1, width), jnp.int32),
            pltpu.SMEM((n_dev, 1, width), jnp.int32),
            pltpu.VMEM(filt.shape, BF16),
            pltpu.VMEM((2, rows, win), BF16),
            pltpu.VMEM((rows * (ups // LANES) + 8, LANES), F32),
            pltpu.VMEM((rows * (band // LANES + 1), LANES), F32),
            pltpu.VMEM((rows, band + LANES), BF16),
            pltpu.VMEM((2, n_rows), F32),
            pltpu.VMEM((n_tile, 2, n_rows), F32),
            pltpu.SemaphoreType.REGULAR,
            sem((6,)),
            sem,
            sem,
            sem((2,)),
            sem((2, n_pulse)),
            sem((2,)),
            sem((3,)),
            sem((3,)),
            sem,
            sem,
        ],
        compiler_params=pltpu.CompilerParams(
            collective_id=0, has_side_effects=True, vmem_limit_bytes=VMEM_LIMIT
        ),
    )(*[pltpu.with_memory_space_constraint(a, pltpu.HBM) for a in (range_off, fine, dop, order, idx, raw, filt)])


def image_kernel(parts, left_ref, samp_ref, out_ref, res_ref, sem):
    r_dev = out_ref.shape[1]
    width = out_ref.shape[2] // parts
    for i in range(parts):
        cols = pl.ds(i * width, width)
        res = jnp.dot(left_ref[...], samp_ref[:, cols], preferred_element_type=F32).astype(BF16)
        for z in range(2):
            res_ref[z, :, cols] = res[z * r_dev : (z + 1) * r_dev]
        pltpu.make_async_copy(res_ref.at[:, :, cols], out_ref.at[:, :, cols], sem).start()
    pltpu.make_async_copy(res_ref, out_ref, sem).wait()


def image(left, samples, r_dev):
    cols = samples.shape[1]
    return pl.pallas_call(
        functools.partial(image_kernel, 8),
        out_shape=jax.ShapeDtypeStruct((2, r_dev, cols), BF16),
        in_specs=[pl.BlockSpec(memory_space=pltpu.VMEM)] * 2,
        out_specs=pl.BlockSpec(memory_space=pltpu.HBM),
        scratch_shapes=[pltpu.VMEM((2, r_dev, cols), BF16), pltpu.SemaphoreType.DMA],
        compiler_params=pltpu.CompilerParams(vmem_limit_bytes=IMAGE_VMEM),
    )(left, samples)


BAND = 1024
R_DEV = 128


def shards(raw, filt, range_off, fine, dop, pulse_order, band_idx):
    n_pulse = lax.axis_size("pulse")
    n_tile = lax.axis_size("tile")
    left, samples = focus(
        n_pulse, n_tile, R_DEV, BAND, range_off, fine, dop, pulse_order, band_idx.T, raw, filt
    )
    return image(left, samples, R_DEV)


def solution(mesh):
    return jax.shard_map(
        shards,
        mesh=mesh,
        in_specs=(
            P(None, ("pulse", "tile"), None),
            P(),
            P(("pulse", "tile")),
            P(("pulse", "tile")),
            P(("pulse", "tile")),
            P(("pulse", "tile"), None),
            P(None, ("pulse", "tile")),
        ),
        out_specs=P(None, "pulse", "tile"),
        check_vma=False,
    )
```
